128 devices in a mesh: section: 2 (over x_lo), patch: 64 (over y, x_hi, z, core).
Axes of the slice: x: 4 (x_hi: 2, x_lo: 2; x = x_hi * 2 + x_lo), y: 4, z: 4, core: 2. Of those that a mesh axis runs over, the one named last changes fastest.
Arguments:
- latents: bfloat16 [2048, 1536], P('patch'), may hold values from -6 to 6
- modulation: float32 [2, 3, 1536], P('section'), may hold values from -3 to 3
- w_query: bfloat16 [2, 1536, 1536], P('section'), may hold values from -0.3125 to 0.3125
- w_key: bfloat16 [2, 1536, 1536], P('section'), may hold values from -0.15625 to 0.15625
- w_value: bfloat16 [2, 1536, 1536], P('section'), may hold values from -0.15625 to 0.15625
- w_out: bfloat16 [2, 1536, 1536], P('section'), may hold values from -0.15625 to 0.15625
- stale_kv: bfloat16 [2, 2048, 2, 1536], P('section', 'patch'), as said below
- order: int32 [64, 4], P('patch'), may hold values from 0 to 3, each once within a row
- final_mod: float32 [2, 1536], replicated, may hold values from -3 to 3
- w_final: bfloat16 [1536, 64], replicated, may hold values from -0.15625 to 0.15625
- tile_map: int32 [128], P(('section', 'patch')), may hold values from 0 to 127, each once
Outputs:
- fresh_kv: bfloat16 [2, 2048, 2, 1536], P('section', 'patch')
- vae_tiles: bfloat16 [128, 24, 64], P(('section', 'patch'))
The draws below stay inside these ranges and needn't reach their ends.
Inputs may be any that keep to these rules, and one draw needn't show every extreme that they name: `order`: each row is a permutation of 0 .. 3. `tile_map`: every tile goes to exactly one device. `stale_kv`: finite values.
All inputs are finite; a program needn't handle non-finite values.
Results may differ from the reference program's by a relative error of at most 0.018.
The reference program's roundings to bfloat16 on the way count: a program that leaves them out, or rounds other values in their place, can miss the bound.
Values may be sent and summed in bfloat16 or wider, within the bound.
No kernel may reach another device: no remote copies, remote signals or barrier semaphores. Data moves between devices by JAX's collectives and lax.ppermute only.
A program may use at most 128 MiB of HBM per device.

```python
import jax
import jax.numpy as jnp
from jax import lax

HEADS = 12
HD = 128
D = 1536
LAT = 64
BLOCKS = 4
BLOCK_TOK = 8
HALO = 4
SECTIONS = 2
PATCH_DEVS = 64
TOKENS = 2048
TILE_TOK = 16
DEVICES = 128


def draw_stale_kv(key, part):
    first_key = jax.random.fold_in(jax.random.fold_in(key, 17), 0)
    base = jax.random.normal(first_key, (SECTIONS, TOKENS, 2, D), jnp.float32)
    return base.astype(jnp.bfloat16)


def steps_of(own_key, extent, pieces, low, high):
    def one(dim, blocks):
        steps = jax.random.uniform(jax.random.fold_in(jax.random.fold_in(own_key, 6), dim), (blocks,), jnp.float32, low / len(pieces), high / len(pieces))
        return jnp.repeat(jnp.exp(steps), extent[dim] // blocks).reshape((-1,) + (1,) * (len(extent) - dim - 1))

    loudness = one(*pieces[0])
    for cut in pieces[1:]:
        loudness = loudness * one(*cut)
    return loudness


def scatter_about(own_key, shape, scale, reach, cuts=(), kind=jnp.bfloat16):
    result = scale * jax.random.normal(own_key, shape, jnp.float32)
    if cuts:
        result = result * steps_of(own_key, shape, cuts, -0.22, 0.18)
    return jnp.clip(result, -reach, reach).astype(kind)


def setup_inputs(seed: int = 0) -> dict:
    streams_of = jax.random.split(jax.random.key(seed), 12)
    return {
        "latents": scatter_about(streams_of[0], (TOKENS, D), 1.0, 6.0, ((0, 64),)),
        "modulation": scatter_about(streams_of[1], (SECTIONS, 3, D), 0.5, 3.0, ((0, 2),), jnp.float32),
        "w_query": scatter_about(streams_of[2], (SECTIONS, D, D), (D // 4) ** -0.5, 0.3125, ((0, 2),)),
        "w_key": scatter_about(streams_of[3], (SECTIONS, D, D), D ** -0.5, 0.15625, ((0, 2),)),
        "w_value": scatter_about(streams_of[4], (SECTIONS, D, D), D ** -0.5, 0.15625, ((0, 2),)),
        "w_out": scatter_about(streams_of[5], (SECTIONS, D, D), D ** -0.5, 0.15625, ((0, 2),)),
        "stale_kv": draw_stale_kv(jax.random.fold_in(streams_of[11], 71), 0),
        "order": jax.vmap(lambda own: jax.random.permutation(own, BLOCKS))(jax.random.split(streams_of[7], PATCH_DEVS)).reshape((PATCH_DEVS, BLOCKS)).astype(jnp.int32),
        "final_mod": scatter_about(streams_of[8], (2, D), 0.5, 3.0, (), jnp.float32),
        "w_final": scatter_about(streams_of[9], (D, LAT), D ** -0.5, 0.15625),
        "tile_map": jax.random.permutation(streams_of[10], DEVICES).astype(jnp.int32),
    }


def layer_norm(hidden):
    values = hidden.astype(jnp.float32)
    center = lax.optimization_barrier(jnp.mean(values, axis=-1, keepdims=True))
    spread = lax.optimization_barrier(jnp.mean((values - center) ** 2, axis=-1, keepdims=True))
    return (values - center) * lax.rsqrt(spread + 1e-06)

def reference(latents, modulation, w_query, w_key, w_value, w_out, stale_kv, order, final_mod, w_final, tile_map):
    per_dev = BLOCKS * BLOCK_TOK
    ranks = lax.optimization_barrier(jnp.sum(jnp.arange(BLOCKS, dtype=jnp.int32)[None, :, None] * (order[:, :, None] == jnp.arange(BLOCKS, dtype=jnp.int32)[None, None, :]).astype(jnp.int32), axis=1)).astype(jnp.int32)
    hidden = latents
    fresh_all = []
    for section_step in range(SECTIONS):
        shift_row = modulation[section_step, 0]
        scale_row = modulation[section_step, 1]
        gate_row = modulation[section_step, 2]
        normed = (layer_norm(hidden) * (1.0 + scale_row) + shift_row).astype(jnp.bfloat16)
        queries = jnp.dot(normed, w_query[section_step], preferred_element_type=jnp.float32).astype(jnp.bfloat16)
        key_rows = jnp.dot(normed, w_key[section_step], preferred_element_type=jnp.float32).astype(jnp.bfloat16)
        value_rows = jnp.dot(normed, w_value[section_step], preferred_element_type=jnp.float32).astype(jnp.bfloat16)
        fresh = jnp.stack([key_rows, value_rows], axis=1)
        selected = stale_kv[section_step]
        keys_all = selected[:, 0].astype(jnp.float32).reshape(TOKENS, HEADS, HD)
        values_all = selected[:, 1].astype(jnp.float32).reshape(TOKENS, HEADS, HD)
        column_dev = jnp.arange(TOKENS, dtype=jnp.int32) // per_dev

        def per_device(patch_id):
            start = (patch_id * per_dev).astype(jnp.int32)
            query_blk = lax.dynamic_slice_in_dim(queries, start, per_dev, 0).astype(jnp.float32).reshape(BLOCKS, BLOCK_TOK, HEADS, HD)
            fresh_own = lax.dynamic_slice_in_dim(fresh, start, per_dev, 0).reshape(BLOCKS, BLOCK_TOK, 2, D)
            stale_own = lax.dynamic_slice_in_dim(selected, start, per_dev, 0).reshape(BLOCKS, BLOCK_TOK, 2, D)
            own_rank = lax.dynamic_index_in_dim(ranks, patch_id, 0, keepdims=False)
            use_fresh = own_rank[None, :] <= own_rank[:, None]
            local = jnp.where(use_fresh[:, :, None, None, None], fresh_own[None], stale_own[None])
            local_keys = local[:, :, :, 0].astype(jnp.float32).reshape(BLOCKS, per_dev, HEADS, HD)
            local_vals = local[:, :, :, 1].astype(jnp.float32).reshape(BLOCKS, per_dev, HEADS, HD)
            remote_scores = jnp.einsum('bthd,khd->bhtk', query_blk, keys_all) * HD ** (-0.5)
            remote_scores = jnp.where((column_dev != patch_id)[None, None, None, :], remote_scores, -1e+30)
            local_scores = jnp.einsum('bthd,bkhd->bhtk', query_blk, local_keys) * HD ** (-0.5)
            row_max = jnp.maximum(lax.optimization_barrier(jnp.max(remote_scores, axis=-1)), lax.optimization_barrier(jnp.max(local_scores, axis=-1)))
            remote_w = jnp.exp(remote_scores - row_max[..., None])
            local_w = jnp.exp(local_scores - row_max[..., None])
            row_total = lax.optimization_barrier(jnp.sum(remote_w, axis=-1)) + lax.optimization_barrier(jnp.sum(local_w, axis=-1))
            remote_p = (remote_w / row_total[..., None]).astype(jnp.bfloat16).astype(jnp.float32)
            local_p = (local_w / row_total[..., None]).astype(jnp.bfloat16).astype(jnp.float32)
            attended = jnp.einsum('bhtk,khd->bthd', remote_p, values_all) + jnp.einsum('bhtk,bkhd->bthd', local_p, local_vals)
            return attended.reshape(per_dev, D)
        attended = lax.map(per_device, jnp.arange(PATCH_DEVS, dtype=jnp.int32)).reshape(TOKENS, D).astype(jnp.bfloat16)
        branch = jnp.dot(attended, w_out[section_step], preferred_element_type=jnp.float32)
        hidden = (hidden.astype(jnp.float32) + gate_row * branch).astype(jnp.bfloat16)
        fresh_all.append(fresh)
    final_normed = (layer_norm(hidden) * (1.0 + final_mod[1]) + final_mod[0]).astype(jnp.bfloat16)
    latent_rows = jnp.dot(final_normed, w_final, preferred_element_type=jnp.float32).astype(jnp.bfloat16)
    padded = jnp.pad(latent_rows, ((HALO, HALO), (0, 0)))

    def take_tile(tile_id):
        return lax.dynamic_slice(padded, ((tile_id * TILE_TOK).astype(jnp.int32), jnp.zeros((), jnp.int32)), (TILE_TOK + 2 * HALO, LAT))
    vae_tiles = lax.map(take_tile, tile_map)
    return (jnp.stack(fresh_all, axis=0), vae_tiles)
```

```python
import functools

import jax
import jax.numpy as jnp
from jax import lax
from jax.experimental import pallas as pl
from jax.experimental.pallas import tpu as pltpu
from jax.sharding import PartitionSpec as P

HD = 128
LOG2E = 1.4426950408889634
MASKED = -1e30


DIMS = {"y": (4, 16), "xh": (2, 8), "z": (4, 2), "c": (2, 1)}
PATCHES = 64


def moved(block, dim, target):
    size, stride = DIMS[dim]
    route = []
    for p in range(PATCHES):
        i = p // stride % size
        route.append((p, p + (target(i) - i) * stride))
    return lax.ppermute(block, "patch", route)


def even_pair(i):
    return i ^ 1


def odd_pair(i):
    return (i + 1) % 4 if i % 2 else (i - 1) % 4


FIRST = ("z", even_pair)
LINKS = (("z", odd_pair), ("y", even_pair), ("xh", even_pair), ("y", odd_pair))


def swapped(block):
    return moved(block, "c", even_pair)


def doubled(parts, step):
    return [moved(part, *LINKS[(i + step) % len(LINKS)]) for i, part in enumerate(parts)]


def joined(parts, got):
    return [jnp.concatenate(pair, axis=0) for pair in zip(parts, got)]


def held_until(values, *done):
    return lax.optimization_barrier((values, done))[0]


def normed_rows(values, scale_row, shift_row):
    center = jnp.mean(values, axis=-1, keepdims=True)
    away = values - center
    spread = jnp.mean(away * away, axis=-1, keepdims=True)
    return (away * lax.rsqrt(spread + 1e-06) * (1.0 + scale_row) + shift_row).astype(jnp.bfloat16)


def call(body, outs, name, limit_mib, *args, **kw):
    return pl.pallas_call(
        body,
        in_specs=kw.pop("in_specs", [pl.BlockSpec(memory_space=pltpu.VMEM) for _ in args]),
        out_specs=[pl.BlockSpec(memory_space=pltpu.VMEM) for _ in outs],
        out_shape=outs,
        compiler_params=pltpu.CompilerParams(vmem_limit_bytes=limit_mib << 20),
        name=name,
        **kw,
    )(*args)


def core_index():
    return lax.rem(lax.axis_index("patch"), 2)


def array(shape, dtype):
    return jax.ShapeDtypeStruct(shape, dtype)


def stale_body(kv_ref, mine_ref, theirs_ref):
    half = mine_ref.shape[1] // 2
    for out_ref, which in ((mine_ref, core_index()), (theirs_ref, 1 - core_index())):
        for h in range(half // HD):
            at = pl.multiple_of(which * half + h * HD, HD)
            for i in range(2):
                out_ref[:, (2 * h + i) * HD : (2 * h + i + 1) * HD] = kv_ref[:, i, pl.ds(at, HD)]


def stale_halves(kv):
    out = array((kv.shape[0], kv.shape[2]), kv.dtype)
    return call(stale_body, [out, out], "stale", 4, kv)


def masks_body(own_ref, other_ref, fresh_ref, stale_ref):
    blocks = own_ref.shape[1]
    rows = fresh_ref.shape[0]
    per_dev = rows // 2

    def side_and_rank(token):
        block = token % per_dev // (per_dev // blocks)
        rank = jnp.zeros_like(token)
        for ref, side in ((own_ref, token < per_dev), (other_ref, token >= per_dev)):
            for t in range(blocks):
                rank = jnp.where(side & (block == ref[0, t]), t, rank)
        return token // per_dev, rank

    query_side, query_rank = side_and_rank(lax.broadcasted_iota(jnp.int32, (rows, HD), 0))
    for i, first in enumerate((0, per_dev)):
        column = lax.broadcasted_iota(jnp.int32, (rows, HD), 1)
        key_side, key_rank = side_and_rank(column % per_dev + first)
        fresh = (key_side == query_side) & (key_rank <= query_rank)
        stale_ref[i] = jnp.where(fresh & (column < per_dev), MASKED, 0.0)
    key_side, key_rank = side_and_rank(lax.broadcasted_iota(jnp.int32, (rows, rows), 1))
    fresh = (key_side == query_side[:, :rows]) & (key_rank <= query_rank[:, :rows])
    fresh_ref[...] = jnp.where(fresh, 0.0, MASKED)


def masks(order, other_order, rows):
    return call(
        masks_body,
        [array((rows, rows), jnp.float32), array((2, rows, HD), jnp.float32)],
        "masks",
        2,
        order,
        other_order,
        in_specs=[pl.BlockSpec(memory_space=pltpu.SMEM)] * 2,
    )


def chosen_body(k1_ref, v1_ref, k2_ref, v2_ref, mine_ref, send_ref):
    rows, half = mine_ref.shape[0], k1_ref.shape[1]
    section = lax.axis_index("section")
    for i, (first, second) in enumerate(((k1_ref, k2_ref), (v1_ref, v2_ref))):
        cols = slice(i * half, (i + 1) * half)

        @pl.when(section == 0)
        def _():
            mine_ref[:, cols] = first[:rows]
            send_ref[:, cols] = first[rows:]

        @pl.when(section != 0)
        def _():
            mine_ref[:, cols] = second[:rows]
            send_ref[:, cols] = second[rows:]


def chosen(*pairs):
    rows, half = pairs[0].shape
    out = array((rows // 2, 2 * half), pairs[0].dtype)
    return call(chosen_body, [out, out], "chosen", 2, *pairs)


def qkv_body(h_ref, g_ref, mod_ref, wq_ref, wk_ref, wv_ref, q_ref, k_ref, v_ref):
    half = q_ref.shape[1]
    cols = pl.ds(pl.multiple_of(core_index() * half, HD), half)
    sides = [
        normed_rows(ref[...].astype(jnp.float32), mod_ref[1], mod_ref[0]) for ref in (h_ref, g_ref)
    ]
    rows = jnp.concatenate(sides, axis=0)
    for w_ref, out_ref in ((wq_ref, q_ref), (wk_ref, k_ref), (wv_ref, v_ref)):
        out_ref[...] = jnp.dot(rows, w_ref[0, :, cols], preferred_element_type=jnp.float32).astype(
            jnp.bfloat16
        )


def qkv(rows, other_rows, mod, wq, wk, wv):
    out = array((2 * rows.shape[0], wq.shape[2] // 2), jnp.bfloat16)
    args = (rows, other_rows, mod, wq, wk, wv)
    return call(qkv_body, [out] * 3, "qkv", 18, *args)


def attend_body(heads, count, first, last, *refs):
    q_ref = refs[0]
    pieces, refs = refs[1 : 1 + count], refs[1 + count :]
    if first:
        (k_ref, v_ref, bias_f_ref, bias_s_ref), refs = refs[:4], refs[4:]
    else:
        (acc_in, top_in, total_in), refs = refs[:3], refs[3:]
    if last:
        w_ref, own_ref, other_ref, att = refs
    else:
        acc_out, top_out, total_out = refs
    factor = HD ** (-0.5) * LOG2E
    for h in range(heads):
        cols = slice(h * HD, (h + 1) * HD)
        q = q_ref[:, cols]

        def product(rows):
            return lax.dot_general(
                q, rows, (((1,), (1,)), ((), ())), preferred_element_type=jnp.float32
            )

        scores, values = [], []
        if first:
            scores.append(product(k_ref[:, cols]) + bias_f_ref[...])
            values.append(v_ref[:, cols])
        at = 2 * HD * h
        for i, piece in enumerate(pieces):
            s = product(piece[:, at : at + HD])
            if first and i < bias_s_ref.shape[0]:
                s = jnp.concatenate([s[:, :HD] + bias_s_ref[i], s[:, HD:]], axis=1)
            scores.append(s)
            values.append(piece[:, at + HD : at + 2 * HD])
        top = functools.reduce(jnp.maximum, [jnp.max(s, axis=-1, keepdims=True) for s in scores])
        if first:
            total, out = 0.0, 0.0
        else:
            before = top_in[:, h : h + 1]
            top = jnp.maximum(top, before)
            scale = jnp.exp2((before - top) * factor)
            total = total_in[:, h : h + 1] * scale
            out = acc_in[:, cols] * scale
        for s, v in zip(scores, values):
            w = jnp.exp2((s - top) * factor)
            total = total + jnp.sum(w, axis=-1, keepdims=True)
            out = out + jnp.dot(w.astype(jnp.bfloat16), v, preferred_element_type=jnp.float32)
        if last:
            att[:, cols] = (out / total).astype(jnp.bfloat16)
        else:
            acc_out[:, cols] = out
            top_out[:, h : h + 1] = top
            total_out[:, h : h + 1] = total
    if last:
        rows = own_ref.shape[0]
        half = att.shape[1]
        w = w_ref[0, pl.ds(pl.multiple_of(core_index() * half, HD), half), :]
        branch = jnp.dot(att[...], w, preferred_element_type=jnp.float32)
        own_ref[...] = branch[:rows]
        other_ref[...] = branch[rows:]


def attend(q, pieces, start, w_out):
    rows, half = q.shape
    heads = half // HD
    first, last = len(start) == 4, w_out is not None
    body = functools.partial(attend_body, heads, len(pieces), first, last)
    args = (q, *pieces, *start)
    if not last:
        state = [array((rows, half), jnp.float32)] + [array((rows, HD), jnp.float32)] * 2
        return call(body, state, "attend_early", 14, *args)
    out = array((rows // 2, w_out.shape[2]), jnp.float32)
    att = pltpu.VMEM((rows, half), jnp.bfloat16)
    return call(body, [out, out], "attend", 16, *args, w_out, scratch_shapes=[att])


def added(h_ref, own_ref, got_ref, mod_ref):
    hidden = h_ref[...].astype(jnp.float32) + mod_ref[2] * (own_ref[...] + got_ref[...])
    return hidden.astype(jnp.bfloat16)


def residual_body(h_ref, own_ref, got_ref, mod_ref, out_ref):
    out_ref[...] = added(h_ref, own_ref, got_ref, mod_ref)


def final_body(h_ref, own_ref, got_ref, mod_ref, fmod_ref, w_ref, out_ref):
    hidden = added(h_ref, own_ref, got_ref, mod_ref).astype(jnp.float32)
    rows = normed_rows(hidden, fmod_ref[1:2, :], fmod_ref[0:1, :])
    latent = lax.dot_general(
        rows, w_ref[...], (((1,), (1,)), ((), ())), preferred_element_type=jnp.float32
    )
    n = latent.shape[0] // 2
    packed = jnp.concatenate([latent[:n], latent[n:]], axis=1).astype(jnp.bfloat16)
    for i in range(out_ref.shape[0]):
        out_ref[i] = packed


def per_device(
    latents,
    modulation,
    w_query,
    w_key,
    w_value,
    w_out,
    stale_kv,
    order,
    final_mod,
    w_final,
    tile_map,
):
    patch = lax.axis_index("patch")
    core = patch % 2
    per_dev, width = latents.shape
    half = width // 2
    blocks = order.shape[1]

    mine, theirs = stale_halves(stale_kv[0])
    parts = [mine, swapped(theirs)]
    parts = lax.optimization_barrier(parts + [moved(part, *FIRST) for part in parts])
    parts = joined(parts, doubled(parts, 0))
    latents, order = held_until((latents, order), parts[-1])

    bias_f, bias_s = masks(order, swapped(order), 2 * per_dev)
    other_latents = swapped(latents)

    parts = joined(parts, doubled(parts, 1))
    early = joined(parts, doubled(parts, 2))
    late = doubled(early, 3)

    mod = jnp.transpose(modulation, (1, 0, 2))
    weights = (w_query, w_key, w_value)
    q, k_first, v_first = qkv(latents, other_latents, mod, *weights)
    state = attend(q, early, (k_first, v_first, bias_f, bias_s), None)
    own, other = attend(q, late, state, w_out)
    (hidden,) = call(
        residual_body, [array(latents.shape, latents.dtype)], "residual", 4, latents, own, swapped(other), mod
    )
    hidden = lax.ppermute(hidden, "section", [(0, 1)])
    q, k_second, v_second = qkv(hidden, swapped(hidden), mod, *weights)
    own, other = attend(q, early + late, (k_second, v_second, bias_f, bias_s), w_out)

    kv_mine, send = chosen(k_first, v_first, k_second, v_second)
    kv_mine = kv_mine.reshape(per_dev, 2, half)
    kv_other = swapped(send).reshape(per_dev, 2, half)
    fresh = jnp.where(
        core == 0,
        jnp.concatenate([kv_mine, kv_other], axis=2),
        jnp.concatenate([kv_other, kv_mine], axis=2),
    )

    lat = w_final.shape[1]
    tok = per_dev // 2
    (copies,) = call(
        final_body,
        [pltpu.VMEM((2 * PATCHES, tok, 2 * lat), jnp.bfloat16)],
        "final",
        6,
        hidden,
        own,
        swapped(other),
        mod,
        final_mod,
        w_final.T,
    )
    rows = lax.all_to_all(copies.reshape(-1, 2 * lat), ("section", "patch"), 0, 0, tiled=True)
    rows = rows.reshape(2 * PATCHES, tok, 2 * lat)[PATCHES:]
    tile = tile_map[0]

    def tile_rows(t):
        t = jnp.clip(t, 0, 2 * PATCHES - 1)
        block = lax.dynamic_index_in_dim(rows, t // 2, 0, keepdims=False)
        return jnp.where(t % 2 == 0, block[:, :lat], block[:, lat:])

    halo = 4
    before = jnp.where(tile > 0, tile_rows(tile - 1)[tok - halo :], 0)
    after = jnp.where(tile < 2 * PATCHES - 1, tile_rows(tile + 1)[:halo], 0)
    window = jnp.concatenate([before, tile_rows(tile), after], axis=0).astype(jnp.bfloat16)
    return (fresh[None], window[None])


def solution(mesh):
    placed = (
        P("patch", None),
        P("section", None, None),
        P("section", None, None),
        P("section", None, None),
        P("section", None, None),
        P("section", None, None),
        P("section", "patch", None, None),
        P("patch", None),
        P(),
        P(),
        P(("section", "patch")),
    )
    return jax.shard_map(
        per_device,
        mesh=mesh,
        in_specs=placed,
        out_specs=(P("section", "patch", None, None), P(("section", "patch"), None, None)),
        check_vma=False,
    )
```

```python
import functools

import jax
import jax.numpy as jnp
from jax import lax
from jax.experimental import pallas as pl
from jax.experimental.pallas import tpu as pltpu
from jax.sharding import PartitionSpec as P

HD = 128
LOG2E = 1.4426950408889634
MASKED = -1e30


DIMS = {"y": (4, 16), "xh": (2, 8), "z": (4, 2), "c": (2, 1)}
PATCHES = 64


def moved(block, dim, target):
    size, stride = DIMS[dim]
    route = []
    for p in range(PATCHES):
        i = p // stride % size
        route.append((p, p + (target(i) - i) * stride))
    return lax.ppermute(block, "patch", route)


def even_pair(i):
    return i ^ 1


def odd_pair(i):
    return (i + 1) % 4 if i % 2 else (i - 1) % 4


FIRST = ("z", even_pair)
LINKS = (("z", odd_pair), ("y", even_pair), ("y", odd_pair), ("xh", even_pair))


def swapped(block):
    return moved(block, "c", even_pair)


def doubled(parts, step):
    return [moved(part, *LINKS[(i + step) % len(LINKS)]) for i, part in enumerate(parts)]


def joined(parts, got):
    return [jnp.concatenate(pair, axis=0) for pair in zip(parts, got)]


def held_until(values, *done):
    return lax.optimization_barrier((values, done))[0]


def normed_rows(values, scale_row, shift_row):
    center = jnp.mean(values, axis=-1, keepdims=True)
    away = values - center
    spread = jnp.mean(away * away, axis=-1, keepdims=True)
    return (away * lax.rsqrt(spread + 1e-06) * (1.0 + scale_row) + shift_row).astype(jnp.bfloat16)


def call(body, outs, name, limit_mib, *args, **kw):
    return pl.pallas_call(
        body,
        in_specs=kw.pop("in_specs", [pl.BlockSpec(memory_space=pltpu.VMEM) for _ in args]),
        out_specs=[pl.BlockSpec(memory_space=pltpu.VMEM) for _ in outs],
        out_shape=outs,
        compiler_params=pltpu.CompilerParams(vmem_limit_bytes=limit_mib << 20),
        name=name,
        **kw,
    )(*args)


def core_index():
    return lax.rem(lax.axis_index("patch"), 2)


def array(shape, dtype):
    return jax.ShapeDtypeStruct(shape, dtype)


def stale_body(kv_ref, mine_ref, theirs_ref):
    half = mine_ref.shape[1] // 2
    for out_ref, which in ((mine_ref, core_index()), (theirs_ref, 1 - core_index())):
        for h in range(half // HD):
            at = pl.multiple_of(which * half + h * HD, HD)
            for i in range(2):
                out_ref[:, (2 * h + i) * HD : (2 * h + i + 1) * HD] = kv_ref[:, i, pl.ds(at, HD)]


def stale_halves(kv):
    out = array((kv.shape[0], kv.shape[2]), kv.dtype)
    return call(stale_body, [out, out], "stale", 4, kv)


def masks_body(own_ref, other_ref, fresh_ref, stale_ref):
    blocks = own_ref.shape[1]
    rows = fresh_ref.shape[0]
    per_dev = rows // 2

    def side_and_rank(token):
        block = token % per_dev // (per_dev // blocks)
        rank = jnp.zeros_like(token)
        for ref, side in ((own_ref, token < per_dev), (other_ref, token >= per_dev)):
            for t in range(blocks):
                rank = jnp.where(side & (block == ref[0, t]), t, rank)
        return token // per_dev, rank

    query_side, query_rank = side_and_rank(lax.broadcasted_iota(jnp.int32, (rows, HD), 0))
    for i, first in enumerate((0, per_dev)):
        column = lax.broadcasted_iota(jnp.int32, (rows, HD), 1)
        key_side, key_rank = side_and_rank(column % per_dev + first)
        fresh = (key_side == query_side) & (key_rank <= query_rank)
        stale_ref[i] = jnp.where(fresh & (column < per_dev), MASKED, 0.0)
    key_side, key_rank = side_and_rank(lax.broadcasted_iota(jnp.int32, (rows, rows), 1))
    fresh = (key_side == query_side[:, :rows]) & (key_rank <= query_rank[:, :rows])
    fresh_ref[...] = jnp.where(fresh, 0.0, MASKED)


def masks(order, other_order, rows):
    return call(
        masks_body,
        [array((rows, rows), jnp.float32), array((2, rows, HD), jnp.float32)],
        "masks",
        2,
        order,
        other_order,
        in_specs=[pl.BlockSpec(memory_space=pltpu.SMEM)] * 2,
    )


def chosen_body(k1_ref, v1_ref, k2_ref, v2_ref, mine_ref, send_ref):
    rows, half = mine_ref.shape[0], k1_ref.shape[1]
    section = lax.axis_index("section")
    for i, (first, second) in enumerate(((k1_ref, k2_ref), (v1_ref, v2_ref))):
        cols = slice(i * half, (i + 1) * half)

        @pl.when(section == 0)
        def _():
            mine_ref[:, cols] = first[:rows]
            send_ref[:, cols] = first[rows:]

        @pl.when(section != 0)
        def _():
            mine_ref[:, cols] = second[:rows]
            send_ref[:, cols] = second[rows:]


def chosen(*pairs):
    rows, half = pairs[0].shape
    out = array((rows // 2, 2 * half), pairs[0].dtype)
    return call(chosen_body, [out, out], "chosen", 2, *pairs)


def qkv_body(h_ref, g_ref, mod_ref, wq_ref, wk_ref, wv_ref, q_ref, k_ref, v_ref):
    half = q_ref.shape[1]
    cols = pl.ds(pl.multiple_of(core_index() * half, HD), half)
    sides = [
        normed_rows(ref[...].astype(jnp.float32), mod_ref[1], mod_ref[0]) for ref in (h_ref, g_ref)
    ]
    rows = jnp.concatenate(sides, axis=0)
    for w_ref, out_ref in ((wq_ref, q_ref), (wk_ref, k_ref), (wv_ref, v_ref)):
        out_ref[...] = jnp.dot(rows, w_ref[0, :, cols], preferred_element_type=jnp.float32).astype(
            jnp.bfloat16
        )


def qkv(rows, other_rows, mod, wq, wk, wv):
    out = array((2 * rows.shape[0], wq.shape[2] // 2), jnp.bfloat16)
    args = (rows, other_rows, mod, wq, wk, wv)
    return call(qkv_body, [out] * 3, "qkv", 18, *args)


def attend_body(heads, count, first, last, *refs):
    q_ref = refs[0]
    pieces, refs = refs[1 : 1 + count], refs[1 + count :]
    if first:
        (k_ref, v_ref, bias_f_ref, bias_s_ref), refs = refs[:4], refs[4:]
    else:
        (acc_in, top_in, total_in), refs = refs[:3], refs[3:]
    if last:
        w_ref, own_ref, other_ref, att = refs
    else:
        acc_out, top_out, total_out = refs
    factor = HD ** (-0.5) * LOG2E
    for h in range(heads):
        cols = slice(h * HD, (h + 1) * HD)
        q = q_ref[:, cols]

        def product(rows):
            return lax.dot_general(
                q, rows, (((1,), (1,)), ((), ())), preferred_element_type=jnp.float32
            )

        scores, values = [], []
        if first:
            scores.append(product(k_ref[:, cols]) + bias_f_ref[...])
            values.append(v_ref[:, cols])
        at = 2 * HD * h
        for i, piece in enumerate(pieces):
            s = product(piece[:, at : at + HD])
            if first and i < bias_s_ref.shape[0]:
                s = jnp.concatenate([s[:, :HD] + bias_s_ref[i], s[:, HD:]], axis=1)
            scores.append(s)
            values.append(piece[:, at + HD : at + 2 * HD])
        top = functools.reduce(jnp.maximum, [jnp.max(s, axis=-1, keepdims=True) for s in scores])
        if first:
            total, out = 0.0, 0.0
        else:
            before = top_in[:, h : h + 1]
            top = jnp.maximum(top, before)
            scale = jnp.exp2((before - top) * factor)
            total = total_in[:, h : h + 1] * scale
            out = acc_in[:, cols] * scale
        for s, v in zip(scores, values):
            w = jnp.exp2((s - top) * factor)
            total = total + jnp.sum(w, axis=-1, keepdims=True)
            out = out + jnp.dot(w.astype(jnp.bfloat16), v, preferred_element_type=jnp.float32)
        if last:
            att[:, cols] = (out / total).astype(jnp.bfloat16)
        else:
            acc_out[:, cols] = out
            top_out[:, h : h + 1] = top
            total_out[:, h : h + 1] = total
    if last:
        rows = own_ref.shape[0]
        half = att.shape[1]
        w = w_ref[0, pl.ds(pl.multiple_of(core_index() * half, HD), half), :]
        branch = jnp.dot(att[...], w, preferred_element_type=jnp.float32)
        own_ref[...] = branch[:rows]
        other_ref[...] = branch[rows:]


def attend(q, pieces, start, w_out):
    rows, half = q.shape
    heads = half // HD
    first, last = len(start) == 4, w_out is not None
    body = functools.partial(attend_body, heads, len(pieces), first, last)
    args = (q, *pieces, *start)
    if not last:
        state = [array((rows, half), jnp.float32)] + [array((rows, HD), jnp.float32)] * 2
        return call(body, state, "attend_early", 14, *args)
    out = array((rows // 2, w_out.shape[2]), jnp.float32)
    att = pltpu.VMEM((rows, half), jnp.bfloat16)
    return call(body, [out, out], "attend", 16, *args, w_out, scratch_shapes=[att])


def added(h_ref, own_ref, got_ref, mod_ref):
    hidden = h_ref[...].astype(jnp.float32) + mod_ref[2] * (own_ref[...] + got_ref[...])
    return hidden.astype(jnp.bfloat16)


def residual_body(h_ref, own_ref, got_ref, mod_ref, out_ref):
    out_ref[...] = added(h_ref, own_ref, got_ref, mod_ref)


def final_body(h_ref, own_ref, got_ref, mod_ref, fmod_ref, w_ref, out_ref):
    hidden = added(h_ref, own_ref, got_ref, mod_ref).astype(jnp.float32)
    rows = normed_rows(hidden, fmod_ref[1:2, :], fmod_ref[0:1, :])
    latent = lax.dot_general(
        rows, w_ref[...], (((1,), (1,)), ((), ())), preferred_element_type=jnp.float32
    )
    n = latent.shape[0] // 2
    packed = jnp.concatenate([latent[:n], latent[n:]], axis=1).astype(jnp.bfloat16)
    for i in range(out_ref.shape[0]):
        out_ref[i] = packed


def per_device(
    latents,
    modulation,
    w_query,
    w_key,
    w_value,
    w_out,
    stale_kv,
    order,
    final_mod,
    w_final,
    tile_map,
):
    patch = lax.axis_index("patch")
    core = patch % 2
    per_dev, width = latents.shape
    half = width // 2
    blocks = order.shape[1]

    mine, theirs = stale_halves(stale_kv[0])
    parts = [mine, swapped(theirs)]
    parts = lax.optimization_barrier(parts + [moved(part, *FIRST) for part in parts])
    parts = joined(parts, doubled(parts, 0))
    latents, order = held_until((latents, order), parts[-1])

    bias_f, bias_s = masks(order, swapped(order), 2 * per_dev)
    other_latents = swapped(latents)

    parts = joined(parts, doubled(parts, 1))
    early = joined(parts, doubled(parts, 2))
    late = doubled(early, 3)

    mod = jnp.transpose(modulation, (1, 0, 2))
    weights = (w_query, w_key, w_value)
    q, k_first, v_first = qkv(latents, other_latents, mod, *weights)
    state = attend(q, early, (k_first, v_first, bias_f, bias_s), None)
    state = attend(q, late[1::2], state, None)
    own, other = attend(q, late[::2], state, w_out)
    (hidden,) = call(
        residual_body, [array(latents.shape, latents.dtype)], "residual", 4, latents, own, swapped(other), mod
    )
    hidden = lax.ppermute(hidden, "section", [(0, 1)])
    q, k_second, v_second = qkv(hidden, swapped(hidden), mod, *weights)
    own, other = attend(q, early + late, (k_second, v_second, bias_f, bias_s), w_out)

    kv_mine, send = chosen(k_first, v_first, k_second, v_second)
    kv_mine = kv_mine.reshape(per_dev, 2, half)
    kv_other = swapped(send).reshape(per_dev, 2, half)
    fresh = jnp.where(
        core == 0,
        jnp.concatenate([kv_mine, kv_other], axis=2),
        jnp.concatenate([kv_other, kv_mine], axis=2),
    )

    lat = w_final.shape[1]
    tok = per_dev // 2
    (copies,) = call(
        final_body,
        [pltpu.VMEM((2 * PATCHES, tok, 2 * lat), jnp.bfloat16)],
        "final",
        6,
        hidden,
        own,
        swapped(other),
        mod,
        final_mod,
        w_final.T,
    )
    rows = lax.all_to_all(copies.reshape(-1, 2 * lat), ("section", "patch"), 0, 0, tiled=True)
    rows = rows.reshape(2 * PATCHES, tok, 2 * lat)[PATCHES:]
    tile = tile_map[0]

    def tile_rows(t):
        t = jnp.clip(t, 0, 2 * PATCHES - 1)
        block = lax.dynamic_index_in_dim(rows, t // 2, 0, keepdims=False)
        return jnp.where(t % 2 == 0, block[:, :lat], block[:, lat:])

    halo = 4
    before = jnp.where(tile > 0, tile_rows(tile - 1)[tok - halo :], 0)
    after = jnp.where(tile < 2 * PATCHES - 1, tile_rows(tile + 1)[:halo], 0)
    window = jnp.concatenate([before, tile_rows(tile), after], axis=0).astype(jnp.bfloat16)
    return (fresh[None], window[None])


def solution(mesh):
    placed = (
        P("patch", None),
        P("section", None, None),
        P("section", None, None),
        P("section", None, None),
        P("section", None, None),
        P("section", None, None),
        P("section", "patch", None, None),
        P("patch", None),
        P(),
        P(),
        P(("section", "patch")),
    )
    return jax.shard_map(
        per_device,
        mesh=mesh,
        in_specs=placed,
        out_specs=(P("section", "patch", None, None), P(("section", "patch"), None, None)),
        check_vma=False,
    )
```

```python
import functools

import jax
import jax.numpy as jnp
from jax import lax
from jax.experimental import pallas as pl
from jax.experimental.pallas import tpu as pltpu
from jax.sharding import PartitionSpec as P

HD = 128
LOG2E = 1.4426950408889634
MASKED = -1e30


DIMS = {"y": (4, 16), "xh": (2, 8), "z": (4, 2), "c": (2, 1)}
PATCHES = 64


def moved(block, dim, target):
    size, stride = DIMS[dim]
    route = []
    for p in range(PATCHES):
        i = p // stride % size
        route.append((p, p + (target(i) - i) * stride))
    return lax.ppermute(block, "patch", route)


def even_pair(i):
    return i ^ 1


def odd_pair(i):
    return (i + 1) % 4 if i % 2 else (i - 1) % 4


FIRST = ("z", even_pair)
LINKS = (("z", odd_pair), ("y", even_pair), ("y", odd_pair), ("xh", even_pair))


def swapped(block):
    return moved(block, "c", even_pair)


def doubled(parts, step):
    return [moved(part, *LINKS[(i + step) % len(LINKS)]) for i, part in enumerate(parts)]


def joined(parts, got):
    return [jnp.concatenate(pair, axis=0) for pair in zip(parts, got)]


def held_until(values, *done):
    return lax.optimization_barrier((values, done))[0]


def normed_rows(values, scale_row, shift_row):
    center = jnp.mean(values, axis=-1, keepdims=True)
    away = values - center
    spread = jnp.mean(away * away, axis=-1, keepdims=True)
    return (away * lax.rsqrt(spread + 1e-06) * (1.0 + scale_row) + shift_row).astype(jnp.bfloat16)


def call(body, outs, name, limit_mib, *args, **kw):
    return pl.pallas_call(
        body,
        in_specs=kw.pop("in_specs", [pl.BlockSpec(memory_space=pltpu.VMEM) for _ in args]),
        out_specs=[pl.BlockSpec(memory_space=pltpu.VMEM) for _ in outs],
        out_shape=outs,
        compiler_params=pltpu.CompilerParams(vmem_limit_bytes=limit_mib << 20),
        name=name,
        **kw,
    )(*args)


def core_index():
    return lax.rem(lax.axis_index("patch"), 2)


def array(shape, dtype):
    return jax.ShapeDtypeStruct(shape, dtype)


def stale_body(kv_ref, mine_ref, theirs_ref):
    half = mine_ref.shape[1] // 2
    for out_ref, which in ((mine_ref, core_index()), (theirs_ref, 1 - core_index())):
        for h in range(half // HD):
            at = pl.multiple_of(which * half + h * HD, HD)
            for i in range(2):
                out_ref[:, (2 * h + i) * HD : (2 * h + i + 1) * HD] = kv_ref[:, i, pl.ds(at, HD)]


def stale_halves(kv):
    out = array((kv.shape[0], kv.shape[2]), kv.dtype)
    return call(stale_body, [out, out], "stale", 4, kv)


def masks_body(own_ref, other_ref, fresh_ref, stale_ref):
    blocks = own_ref.shape[1]
    rows = fresh_ref.shape[0]
    per_dev = rows // 2

    def side_and_rank(token):
        block = token % per_dev // (per_dev // blocks)
        rank = jnp.zeros_like(token)
        for ref, side in ((own_ref, token < per_dev), (other_ref, token >= per_dev)):
            for t in range(blocks):
                rank = jnp.where(side & (block == ref[0, t]), t, rank)
        return token // per_dev, rank

    query_side, query_rank = side_and_rank(lax.broadcasted_iota(jnp.int32, (rows, HD), 0))
    for i, first in enumerate((0, per_dev)):
        column = lax.broadcasted_iota(jnp.int32, (rows, HD), 1)
        key_side, key_rank = side_and_rank(column % per_dev + first)
        fresh = (key_side == query_side) & (key_rank <= query_rank)
        stale_ref[i] = jnp.where(fresh & (column < per_dev), MASKED, 0.0)
    key_side, key_rank = side_and_rank(lax.broadcasted_iota(jnp.int32, (rows, rows), 1))
    fresh = (key_side == query_side[:, :rows]) & (key_rank <= query_rank[:, :rows])
    fresh_ref[...] = jnp.where(fresh, 0.0, MASKED)


def masks(order, other_order, rows):
    return call(
        masks_body,
        [array((rows, rows), jnp.float32), array((2, rows, HD), jnp.float32)],
        "masks",
        2,
        order,
        other_order,
        in_specs=[pl.BlockSpec(memory_space=pltpu.SMEM)] * 2,
    )


def chosen_body(k1_ref, v1_ref, k2_ref, v2_ref, mine_ref, send_ref):
    rows, half = mine_ref.shape[0], k1_ref.shape[1]
    section = lax.axis_index("section")
    for i, (first, second) in enumerate(((k1_ref, k2_ref), (v1_ref, v2_ref))):
        cols = slice(i * half, (i + 1) * half)

        @pl.when(section == 0)
        def _():
            mine_ref[:, cols] = first[:rows]
            send_ref[:, cols] = first[rows:]

        @pl.when(section != 0)
        def _():
            mine_ref[:, cols] = second[:rows]
            send_ref[:, cols] = second[rows:]


def chosen(*pairs):
    rows, half = pairs[0].shape
    out = array((rows // 2, 2 * half), pairs[0].dtype)
    return call(chosen_body, [out, out], "chosen", 2, *pairs)


def qkv_body(h_ref, g_ref, mod_ref, wq_ref, wk_ref, wv_ref, q_ref, k_ref, v_ref):
    half = q_ref.shape[1]
    cols = pl.ds(pl.multiple_of(core_index() * half, HD), half)
    sides = [
        normed_rows(ref[...].astype(jnp.float32), mod_ref[1], mod_ref[0]) for ref in (h_ref, g_ref)
    ]
    rows = jnp.concatenate(sides, axis=0)
    for w_ref, out_ref in ((wq_ref, q_ref), (wk_ref, k_ref), (wv_ref, v_ref)):
        out_ref[...] = jnp.dot(rows, w_ref[0, :, cols], preferred_element_type=jnp.float32).astype(
            jnp.bfloat16
        )


def qkv(rows, other_rows, mod, wq, wk, wv):
    out = array((2 * rows.shape[0], wq.shape[2] // 2), jnp.bfloat16)
    args = (rows, other_rows, mod, wq, wk, wv)
    return call(qkv_body, [out] * 3, "qkv", 18, *args)


def attend_body(heads, count, first, last, *refs):
    q_ref = refs[0]
    pieces, refs = refs[1 : 1 + count], refs[1 + count :]
    if first:
        (k_ref, v_ref, bias_f_ref, bias_s_ref), refs = refs[:4], refs[4:]
    else:
        (acc_in, top_in, total_in), refs = refs[:3], refs[3:]
    if last:
        w_ref, own_ref, other_ref, att = refs
    else:
        acc_out, top_out, total_out = refs
    factor = HD ** (-0.5) * LOG2E
    for h in range(heads):
        cols = slice(h * HD, (h + 1) * HD)
        q = q_ref[:, cols]

        def product(rows):
            return lax.dot_general(
                q, rows, (((1,), (1,)), ((), ())), preferred_element_type=jnp.float32
            )

        scores, values = [], []
        if first:
            scores.append(product(k_ref[:, cols]) + bias_f_ref[...])
            values.append(v_ref[:, cols])
        at = 2 * HD * h
        for i, piece in enumerate(pieces):
            s = product(piece[:, at : at + HD])
            if first and i < bias_s_ref.shape[0]:
                s = jnp.concatenate([s[:, :HD] + bias_s_ref[i], s[:, HD:]], axis=1)
            scores.append(s)
            values.append(piece[:, at + HD : at + 2 * HD])
        top = functools.reduce(jnp.maximum, [jnp.max(s, axis=-1, keepdims=True) for s in scores])
        if first:
            total, out = 0.0, 0.0
        else:
            before = top_in[:, h : h + 1]
            top = jnp.maximum(top, before)
            scale = jnp.exp2((before - top) * factor)
            total = total_in[:, h : h + 1] * scale
            out = acc_in[:, cols] * scale
        for s, v in zip(scores, values):
            w = jnp.exp2((s - top) * factor)
            total = total + jnp.sum(w, axis=-1, keepdims=True)
            out = out + jnp.dot(w.astype(jnp.bfloat16), v, preferred_element_type=jnp.float32)
        if last:
            att[:, cols] = (out / total).astype(jnp.bfloat16)
        else:
            acc_out[:, cols] = out
            top_out[:, h : h + 1] = top
            total_out[:, h : h + 1] = total
    if last:
        rows = own_ref.shape[0]
        half = att.shape[1]
        w = w_ref[0, pl.ds(pl.multiple_of(core_index() * half, HD), half), :]
        branch = jnp.dot(att[...], w, preferred_element_type=jnp.float32)
        own_ref[...] = branch[:rows]
        other_ref[...] = branch[rows:]


def attend(q, pieces, start, w_out):
    rows, half = q.shape
    heads = half // HD
    first, last = len(start) == 4, w_out is not None
    body = functools.partial(attend_body, heads, len(pieces), first, last)
    args = (q, *pieces, *start)
    if not last:
        state = [array((rows, half), jnp.float32)] + [array((rows, HD), jnp.float32)] * 2
        return call(body, state, "attend_early", 14, *args)
    out = array((rows // 2, w_out.shape[2]), jnp.float32)
    att = pltpu.VMEM((rows, half), jnp.bfloat16)
    return call(body, [out, out], "attend", 16, *args, w_out, scratch_shapes=[att])


def added(h_ref, own_ref, got_ref, mod_ref):
    hidden = h_ref[...].astype(jnp.float32) + mod_ref[2] * (own_ref[...] + got_ref[...])
    return hidden.astype(jnp.bfloat16)


def residual_body(h_ref, own_ref, got_ref, mod_ref, out_ref):
    out_ref[...] = added(h_ref, own_ref, got_ref, mod_ref)


def final_body(h_ref, own_ref, got_ref, mod_ref, fmod_ref, w_ref, out_ref):
    hidden = added(h_ref, own_ref, got_ref, mod_ref).astype(jnp.float32)
    rows = normed_rows(hidden, fmod_ref[1:2, :], fmod_ref[0:1, :])
    latent = lax.dot_general(
        rows, w_ref[...], (((1,), (1,)), ((), ())), preferred_element_type=jnp.float32
    )
    n = latent.shape[0] // 2
    packed = jnp.concatenate([latent[:n], latent[n:]], axis=1).astype(jnp.bfloat16)
    for i in range(out_ref.shape[0]):
        out_ref[i] = packed


def per_device(
    latents,
    modulation,
    w_query,
    w_key,
    w_value,
    w_out,
    stale_kv,
    order,
    final_mod,
    w_final,
    tile_map,
):
    patch = lax.axis_index("patch")
    core = patch % 2
    per_dev, width = latents.shape
    half = width // 2
    blocks = order.shape[1]

    mine, theirs = stale_halves(stale_kv[0])
    parts = [mine, swapped(theirs)]
    parts = lax.optimization_barrier(parts + [moved(part, *FIRST) for part in parts])
    parts = joined(parts, doubled(parts, 0))
    latents, order = held_until((latents, order), parts[-1])

    bias_f, bias_s = masks(order, swapped(order), 2 * per_dev)
    other_latents = swapped(latents)

    parts = joined(parts, doubled(parts, 1))
    early = joined(parts, doubled(parts, 2))
    late = doubled(early, 3)

    mod = jnp.transpose(modulation, (1, 0, 2))
    weights = (w_query, w_key, w_value)
    q, k_first, v_first = qkv(latents, other_latents, mod, *weights)
    state = attend(q, early, (k_first, v_first, bias_f, bias_s), None)
    own, other = attend(q, late, state, w_out)
    (hidden,) = call(
        residual_body, [array(latents.shape, latents.dtype)], "residual", 4, latents, own, swapped(other), mod
    )
    hidden = lax.ppermute(hidden, "section", [(0, 1)])
    q, k_second, v_second = qkv(hidden, swapped(hidden), mod, *weights)
    own, other = attend(q, early + late, (k_second, v_second, bias_f, bias_s), w_out)

    kv_mine, send = chosen(k_first, v_first, k_second, v_second)
    kv_mine = kv_mine.reshape(per_dev, 2, half)
    kv_other = swapped(send).reshape(per_dev, 2, half)
    fresh = jnp.where(
        core == 0,
        jnp.concatenate([kv_mine, kv_other], axis=2),
        jnp.concatenate([kv_other, kv_mine], axis=2),
    )

    lat = w_final.shape[1]
    tok = per_dev // 2
    (copies,) = call(
        final_body,
        [pltpu.VMEM((2 * PATCHES, tok, 2 * lat), jnp.bfloat16)],
        "final",
        6,
        hidden,
        own,
        swapped(other),
        mod,
        final_mod,
        w_final.T,
    )
    rows = lax.all_to_all(copies.reshape(-1, 2 * lat), ("section", "patch"), 0, 0, tiled=True)
    rows = rows.reshape(2 * PATCHES, tok, 2 * lat)[PATCHES:]
    tile = tile_map[0]

    def tile_rows(t):
        t = jnp.clip(t, 0, 2 * PATCHES - 1)
        block = lax.dynamic_index_in_dim(rows, t // 2, 0, keepdims=False)
        return jnp.where(t % 2 == 0, block[:, :lat], block[:, lat:])

    halo = 4
    before = jnp.where(tile > 0, tile_rows(tile - 1)[tok - halo :], 0)
    after = jnp.where(tile < 2 * PATCHES - 1, tile_rows(tile + 1)[:halo], 0)
    window = jnp.concatenate([before, tile_rows(tile), after], axis=0).astype(jnp.bfloat16)
    return (fresh[None], window[None])


def solution(mesh):
    placed = (
        P("patch", None),
        P("section", None, None),
        P("section", None, None),
        P("section", None, None),
        P("section", None, None),
        P("section", None, None),
        P("section", "patch", None, None),
        P("patch", None),
        P(),
        P(),
        P(("section", "patch")),
    )
    return jax.shard_map(
        per_device,
        mesh=mesh,
        in_specs=placed,
        out_specs=(P("section", "patch", None, None), P(("section", "patch"), None, None)),
        check_vma=False,
    )
```

```python
import functools

import jax
import jax.numpy as jnp
from jax import lax
from jax.experimental import pallas as pl
from jax.experimental.pallas import tpu as pltpu
from jax.sharding import PartitionSpec as P

HD = 128
LOG2E = 1.4426950408889634
MASKED = -1e30


DIMS = {"y": (4, 16), "xh": (2, 8), "z": (4, 2), "c": (2, 1)}
PATCHES = 64


def moved(block, dim, target):
    size, stride = DIMS[dim]
    route = []
    for p in range(PATCHES):
        i = p // stride % size
        route.append((p, p + (target(i) - i) * stride))
    return lax.ppermute(block, "patch", route)


def even_pair(i):
    return i ^ 1


def odd_pair(i):
    return (i + 1) % 4 if i % 2 else (i - 1) % 4


FIRST = ("z", even_pair)
LINKS = (("z", odd_pair), ("y", even_pair), ("xh", even_pair), ("y", odd_pair))


def swapped(block):
    return moved(block, "c", even_pair)


def doubled(parts, step):
    return [moved(part, *LINKS[(i + step) % len(LINKS)]) for i, part in enumerate(parts)]


def joined(parts, got):
    return [jnp.concatenate(pair, axis=0) for pair in zip(parts, got)]


def held_until(values, *done):
    return lax.optimization_barrier((values, done))[0]


def normed_rows(values, scale_row, shift_row):
    center = jnp.mean(values, axis=-1, keepdims=True)
    away = values - center
    spread = jnp.mean(away * away, axis=-1, keepdims=True)
    return (away * lax.rsqrt(spread + 1e-06) * (1.0 + scale_row) + shift_row).astype(jnp.bfloat16)


def call(body, outs, name, limit_mib, *args, **kw):
    return pl.pallas_call(
        body,
        in_specs=kw.pop("in_specs", [pl.BlockSpec(memory_space=pltpu.VMEM) for _ in args]),
        out_specs=[pl.BlockSpec(memory_space=pltpu.VMEM) for _ in outs],
        out_shape=outs,
        compiler_params=pltpu.CompilerParams(vmem_limit_bytes=limit_mib << 20),
        name=name,
        **kw,
    )(*args)


def core_index():
    return lax.rem(lax.axis_index("patch"), 2)


def array(shape, dtype):
    return jax.ShapeDtypeStruct(shape, dtype)


def stale_body(kv_ref, mine_ref, theirs_ref):
    half = mine_ref.shape[1] // 2
    for out_ref, which in ((mine_ref, core_index()), (theirs_ref, 1 - core_index())):
        for h in range(half // HD):
            at = pl.multiple_of(which * half + h * HD, HD)
            for i in range(2):
                out_ref[:, (2 * h + i) * HD : (2 * h + i + 1) * HD] = kv_ref[:, i, pl.ds(at, HD)]


def stale_halves(kv):
    out = array((kv.shape[0], kv.shape[2]), kv.dtype)
    return call(stale_body, [out, out], "stale", 4, kv)


def masks_body(own_ref, other_ref, fresh_ref, stale_ref):
    blocks = own_ref.shape[1]
    rows = fresh_ref.shape[0]
    per_dev = rows // 2

    def side_and_rank(token):
        block = token % per_dev // (per_dev // blocks)
        rank = jnp.zeros_like(token)
        for ref, side in ((own_ref, token < per_dev), (other_ref, token >= per_dev)):
            for t in range(blocks):
                rank = jnp.where(side & (block == ref[0, t]), t, rank)
        return token // per_dev, rank

    query_side, query_rank = side_and_rank(lax.broadcasted_iota(jnp.int32, (rows, HD), 0))
    for i, first in enumerate((0, per_dev)):
        column = lax.broadcasted_iota(jnp.int32, (rows, HD), 1)
        key_side, key_rank = side_and_rank(column % per_dev + first)
        fresh = (key_side == query_side) & (key_rank <= query_rank)
        stale_ref[i] = jnp.where(fresh & (column < per_dev), MASKED, 0.0)
    key_side, key_rank = side_and_rank(lax.broadcasted_iota(jnp.int32, (rows, rows), 1))
    fresh = (key_side == query_side[:, :rows]) & (key_rank <= query_rank[:, :rows])
    fresh_ref[...] = jnp.where(fresh, 0.0, MASKED)


def masks(order, other_order, rows):
    return call(
        masks_body,
        [array((rows, rows), jnp.float32), array((2, rows, HD), jnp.float32)],
        "masks",
        2,
        order,
        other_order,
        in_specs=[pl.BlockSpec(memory_space=pltpu.SMEM)] * 2,
    )


def chosen_body(k1_ref, v1_ref, k2_ref, v2_ref, mine_ref, send_ref):
    rows, half = mine_ref.shape[0], k1_ref.shape[1]
    section = lax.axis_index("section")
    for i, (first, second) in enumerate(((k1_ref, k2_ref), (v1_ref, v2_ref))):
        cols = slice(i * half, (i + 1) * half)

        @pl.when(section == 0)
        def _():
            mine_ref[:, cols] = first[:rows]
            send_ref[:, cols] = first[rows:]

        @pl.when(section != 0)
        def _():
            mine_ref[:, cols] = second[:rows]
            send_ref[:, cols] = second[rows:]


def chosen(*pairs):
    rows, half = pairs[0].shape
    out = array((rows // 2, 2 * half), pairs[0].dtype)
    return call(chosen_body, [out, out], "chosen", 2, *pairs)


def qkv_body(h_ref, g_ref, mod_ref, wq_ref, wk_ref, wv_ref, q_ref, k_ref, v_ref):
    half = q_ref.shape[1]
    cols = pl.ds(pl.multiple_of(core_index() * half, HD), half)
    sides = [
        normed_rows(ref[...].astype(jnp.float32), mod_ref[1], mod_ref[0]) for ref in (h_ref, g_ref)
    ]
    rows = jnp.concatenate(sides, axis=0)
    for w_ref, out_ref in ((wq_ref, q_ref), (wk_ref, k_ref), (wv_ref, v_ref)):
        out_ref[...] = jnp.dot(rows, w_ref[0, :, cols], preferred_element_type=jnp.float32).astype(
            jnp.bfloat16
        )


def qkv(rows, other_rows, mod, wq, wk, wv):
    out = array((2 * rows.shape[0], wq.shape[2] // 2), jnp.bfloat16)
    args = (rows, other_rows, mod, wq, wk, wv)
    return call(qkv_body, [out] * 3, "qkv", 18, *args)


def attend_body(heads, count, first, last, *refs):
    q_ref = refs[0]
    pieces, refs = refs[1 : 1 + count], refs[1 + count :]
    if first:
        (k_ref, v_ref, bias_f_ref, bias_s_ref), refs = refs[:4], refs[4:]
    else:
        (acc_in, top_in, total_in), refs = refs[:3], refs[3:]
    if last:
        w_ref, own_ref, other_ref, att = refs
    else:
        acc_out, top_out, total_out = refs
    factor = HD ** (-0.5) * LOG2E
    for h in range(heads):
        cols = slice(h * HD, (h + 1) * HD)
        q = q_ref[:, cols]

        def product(rows):
            return lax.dot_general(
                q, rows, (((1,), (1,)), ((), ())), preferred_element_type=jnp.float32
            )

        scores, values = [], []
        if first:
            scores.append(product(k_ref[:, cols]) + bias_f_ref[...])
            values.append(v_ref[:, cols])
        at = 2 * HD * h
        for i, piece in enumerate(pieces):
            s = product(piece[:, at : at + HD])
            if first and i < bias_s_ref.shape[0]:
                s = jnp.concatenate([s[:, :HD] + bias_s_ref[i], s[:, HD:]], axis=1)
            scores.append(s)
            values.append(piece[:, at + HD : at + 2 * HD])
        top = functools.reduce(jnp.maximum, [jnp.max(s, axis=-1, keepdims=True) for s in scores])
        if first:
            total, out = 0.0, 0.0
        else:
            before = top_in[:, h : h + 1]
            top = jnp.maximum(top, before)
            scale = jnp.exp2((before - top) * factor)
            total = total_in[:, h : h + 1] * scale
            out = acc_in[:, cols] * scale
        for s, v in zip(scores, values):
            w = jnp.exp2((s - top) * factor)
            total = total + jnp.sum(w, axis=-1, keepdims=True)
            out = out + jnp.dot(w.astype(jnp.bfloat16), v, preferred_element_type=jnp.float32)
        if last:
            att[:, cols] = (out / total).astype(jnp.bfloat16)
        else:
            acc_out[:, cols] = out
            top_out[:, h : h + 1] = top
            total_out[:, h : h + 1] = total
    if last:
        rows = own_ref.shape[0]
        half = att.shape[1]
        w = w_ref[0, pl.ds(pl.multiple_of(core_index() * half, HD), half), :]
        branch = jnp.dot(att[...], w, preferred_element_type=jnp.float32)
        own_ref[...] = branch[:rows]
        other_ref[...] = branch[rows:]


def attend(q, pieces, start, w_out):
    rows, half = q.shape
    heads = half // HD
    first, last = len(start) == 4, w_out is not None
    body = functools.partial(attend_body, heads, len(pieces), first, last)
    args = (q, *pieces, *start)
    if not last:
        state = [array((rows, half), jnp.float32)] + [array((rows, HD), jnp.float32)] * 2
        return call(body, state, "attend_early", 14, *args)
    out = array((rows // 2, w_out.shape[2]), jnp.float32)
    att = pltpu.VMEM((rows, half), jnp.bfloat16)
    return call(body, [out, out], "attend", 16, *args, w_out, scratch_shapes=[att])


def added(h_ref, own_ref, got_ref, mod_ref):
    hidden = h_ref[...].astype(jnp.float32) + mod_ref[2] * (own_ref[...] + got_ref[...])
    return hidden.astype(jnp.bfloat16)


def residual_body(h_ref, own_ref, got_ref, mod_ref, out_ref):
    out_ref[...] = added(h_ref, own_ref, got_ref, mod_ref)


def final_body(h_ref, own_ref, got_ref, mod_ref, fmod_ref, w_ref, out_ref):
    hidden = added(h_ref, own_ref, got_ref, mod_ref).astype(jnp.float32)
    rows = normed_rows(hidden, fmod_ref[1:2, :], fmod_ref[0:1, :])
    latent = lax.dot_general(
        rows, w_ref[...], (((1,), (1,)), ((), ())), preferred_element_type=jnp.float32
    )
    n = latent.shape[0] // 2
    packed = jnp.concatenate([latent[:n], latent[n:]], axis=1).astype(jnp.bfloat16)
    for i in range(out_ref.shape[0]):
        out_ref[i] = packed


def per_device(
    latents,
    modulation,
    w_query,
    w_key,
    w_value,
    w_out,
    stale_kv,
    order,
    final_mod,
    w_final,
    tile_map,
):
    patch = lax.axis_index("patch")
    core = patch % 2
    per_dev, width = latents.shape
    half = width // 2
    blocks = order.shape[1]

    mine, theirs = stale_halves(stale_kv[0])
    parts = [mine, swapped(theirs)]
    parts = lax.optimization_barrier(parts + [moved(part, *FIRST) for part in parts])
    parts = joined(parts, doubled(parts, 0))
    latents, order = held_until((latents, order), parts[-1])

    bias_f, bias_s = masks(order, swapped(order), 2 * per_dev)
    other_latents = swapped(latents)

    parts = joined(parts, doubled(parts, 1))
    early = joined(parts, doubled(parts, 2))
    late = doubled(early, 3)

    mod = jnp.transpose(modulation, (1, 0, 2))
    weights = (w_query, w_key, w_value)
    q, k_first, v_first = qkv(latents, other_latents, mod, *weights)
    state = attend(q, early, (k_first, v_first, bias_f, bias_s), None)
    state = attend(q, late[2:], state, None)
    own, other = attend(q, late[:2], state, w_out)
    (hidden,) = call(
        residual_body, [array(latents.shape, latents.dtype)], "residual", 4, latents, own, swapped(other), mod
    )
    hidden = lax.ppermute(hidden, "section", [(0, 1)])
    q, k_second, v_second = qkv(hidden, swapped(hidden), mod, *weights)
    own, other = attend(q, early + late, (k_second, v_second, bias_f, bias_s), w_out)

    kv_mine, send = chosen(k_first, v_first, k_second, v_second)
    kv_mine = kv_mine.reshape(per_dev, 2, half)
    kv_other = swapped(send).reshape(per_dev, 2, half)
    fresh = jnp.where(
        core == 0,
        jnp.concatenate([kv_mine, kv_other], axis=2),
        jnp.concatenate([kv_other, kv_mine], axis=2),
    )

    lat = w_final.shape[1]
    tok = per_dev // 2
    (copies,) = call(
        final_body,
        [pltpu.VMEM((2 * PATCHES, tok, 2 * lat), jnp.bfloat16)],
        "final",
        6,
        hidden,
        own,
        swapped(other),
        mod,
        final_mod,
        w_final.T,
    )
    rows = lax.all_to_all(copies.reshape(-1, 2 * lat), ("section", "patch"), 0, 0, tiled=True)
    rows = rows.reshape(2 * PATCHES, tok, 2 * lat)[PATCHES:]
    tile = tile_map[0]

    def tile_rows(t):
        t = jnp.clip(t, 0, 2 * PATCHES - 1)
        block = lax.dynamic_index_in_dim(rows, t // 2, 0, keepdims=False)
        return jnp.where(t % 2 == 0, block[:, :lat], block[:, lat:])

    halo = 4
    before = jnp.where(tile > 0, tile_rows(tile - 1)[tok - halo :], 0)
    after = jnp.where(tile < 2 * PATCHES - 1, tile_rows(tile + 1)[:halo], 0)
    window = jnp.concatenate([before, tile_rows(tile), after], axis=0).astype(jnp.bfloat16)
    return (fresh[None], window[None])


def solution(mesh):
    placed = (
        P("patch", None),
        P("section", None, None),
        P("section", None, None),
        P("section", None, None),
        P("section", None, None),
        P("section", None, None),
        P("section", "patch", None, None),
        P("patch", None),
        P(),
        P(),
        P(("section", "patch")),
    )
    return jax.shard_map(
        per_device,
        mesh=mesh,
        in_specs=placed,
        out_specs=(P("section", "patch", None, None), P(("section", "patch"), None, None)),
        check_vma=False,
    )
```
